32 devices in a mesh: section: 2 (over core), dp: 4 (over z), expert: 4 (over y, x).
Axes of the slice: x: 2, y: 2, z: 4, core: 2. Of those that a mesh axis runs over, the one named last changes fastest.
Arguments:
- inputs: bfloat16 [2, 2048, 768], P(None, ('dp', 'expert')), may hold values from -6 to 6
- cotangent: bfloat16 [2, 2048, 768], P(None, ('dp', 'expert')), may hold values from -6 to 6
- seq_lengths: int32 [2, 4, 3], P(None, 'dp'), may hold values from 1 to 256, 448 in all within a row
- pack_order: int32 [2, 4, 512], P(None, 'dp'), may hold values from 0 to 511, each once within a row
- routes: int32 [2, 2048, 2], P(None, ('dp', 'expert')), may hold values from 0 to 3, all different within a row; in each aligned block of 128 rows (0 to 127, 128 to 255, ..., all dimensions but the last counted through in order) at most 80 rows name the same one
- attn_gain: bfloat16 [2, 768], P('section'), may hold values from 0.5 to 1.5
- w_qkv: bfloat16 [2, 768, 2304], P('section'), may hold values from -0.21875 to 0.21875
- w_attn_out: bfloat16 [2, 768, 768], P('section'), may hold values from -0.875 to 0.875
- rel_bias: float32 [2, 12, 32], P('section'), may hold values from -4 to 4
- ffn_gain: bfloat16 [2, 768], P('section'), may hold values from 0.5 to 1.5
- w_router: bfloat16 [2, 768, 4], P('section'), may hold values from -0.21875 to 0.21875
- w_in: bfloat16 [2, 4, 768, 3072], P('section', 'expert'), may hold values from -0.21875 to 0.21875
- w_down: bfloat16 [2, 4, 3072, 768], P('section', 'expert'), may hold values from -0.109375 to 0.109375
Outputs:
- acts: bfloat16 [2, 2, 2048, 768], P('section', None, ('dp', 'expert'))
- in_grads: bfloat16 [2, 2, 2048, 768], P('section', None, ('dp', 'expert'))
- grad_attn_gain: float32 [2, 768], P('section')
- grad_w_qkv: float32 [2, 768, 2304], P('section')
- grad_w_attn_out: float32 [2, 768, 768], P('section')
- grad_rel_bias: float32 [2, 12, 32], P('section')
- grad_ffn_gain: float32 [2, 768], P('section')
- grad_router: float32 [2, 768, 4], P('section')
- grad_w_in: float32 [2, 4, 768, 3072], P('section', 'expert', 'dp')
- grad_w_down: float32 [2, 4, 3072, 768], P('section', 'expert', 'dp')
The draws below stay inside these ranges and needn't reach their ends.
Inputs may be any that keep to these rules, and one draw needn't show every extreme that they name: `routes`: in each micro-batch the 128 rows of one device name each expert at most 80 times over both choices; a row's two experts differ. `seq_lengths`: the 3 lengths of one group's micro-batch sum to 448. `pack_order`: for each micro-batch and group a permutation of 0 .. 511.
All inputs are finite; a program needn't handle non-finite values.
Results may differ from the reference program's by a relative error of at most 0.02.
Values may be sent and summed in bfloat16 or wider, within the bound.
No kernel may reach another device: no remote copies, remote signals or barrier semaphores. Data moves between devices by JAX's collectives and lax.ppermute only.
A program may use at most 384 MiB of HBM per device.

```python
import math
import jax
import jax.numpy as jnp
import numpy as np
from jax import lax

D = 768
HEADS = 12
HEAD_DIM = 64
FF = 3072
BUCKETS = 32
MAX_DIST = 128
TOP = 2
MICRO = 2
SEQS = 3
TOK_DEV = 128
SECTIONS = 2
EXPERTS = 4
GROUP_TOK = 512
TOKENS = 2048
SEQ_MOST = 256
PACKED = 448
CAP = 80
N_DP = 4


def shard_levels(rng, extent, pieces, least, top_value):
    factor_of, own = 1.0, jax.random.fold_in(rng, 6)
    for axis_at, blocks in pieces:
        heights = jnp.exp(jax.random.uniform(jax.random.fold_in(own, axis_at), (blocks,), jnp.float32, least / len(pieces), top_value / len(pieces)))
        factor_of = factor_of * jnp.repeat(heights, extent[axis_at] // blocks).reshape([-1 if axis == axis_at else 1 for axis in range(len(extent))])
    return factor_of


def split_up(number_of, total, bound, skew):
    weights = [(1 << 20) // math.isqrt(standing ** skew) + 1 for standing in range(2, number_of + 1)]
    spare, holding = total - bound - (number_of - 1), [1] * (number_of - 1)
    while spare > 0:
        movable = [i for i in range(number_of - 1) if holding[i] < bound]
        whole, remaining = sum([weights[i] for i in movable]), spare
        for i in movable:
            more = min(bound - holding[i], max(1, remaining * weights[i] // whole), spare)
            holding[i] = holding[i] + more
            spare = spare - more
    return np.array([bound] + holding)


def uneven_parts(stream_key, number_of, total, reach, lean):
    if number_of == 2:
        one = jax.random.randint(stream_key, (), max(1, total - reach), min(reach, total - 1) + 1)
        return jnp.stack([one, total - one])
    sizes = jnp.asarray(split_up(number_of, total, reach, lean), jnp.int32)
    couples = (number_of - 1) // 2
    source_of, sink = sizes[1:1 + 2 * couples:2], sizes[2:2 + 2 * couples:2]
    margin = jnp.minimum(source_of - 1, reach - sink)
    moved = jax.random.randint(jax.random.fold_in(stream_key, 1), (couples,), 0, 1 << 20) % (margin + 1)
    sizes = sizes.at[1:1 + 2 * couples:2].set(source_of - moved).at[2:2 + 2 * couples:2].set(sink + moved)
    return sizes[jax.random.permutation(jax.random.fold_in(stream_key, 2), number_of)]


def deal_out(stream_key, own, number, rows, amount, top, most, skew):
    ranking = jax.random.permutation(stream_key, amount)
    crowded, common = portions_of(amount, rows * top, most, skew, True), portions_of(amount, rows * top, most, skew, False)
    places = jnp.arange(amount)

    def named(sizes, rotation):
        used = int((sizes > 0).sum())
        fixed = max(1, used // 4)
        moved = fixed + (places - fixed + rotation * (used - fixed)) % max(1, amount - fixed)
        return jnp.zeros((amount,), jnp.int32).at[ranking[jnp.where(places < fixed, places, moved)]].set(jnp.asarray(sizes, jnp.int32))

    sizes = jnp.where(number % 4 == 0, named(crowded, number // 4), named(common, number - number // 4 - 1))
    mixed = jax.random.permutation(jax.random.fold_in(own, 3), amount)
    source_of, receiver = mixed[0:amount // 2 * 2:2], mixed[1:amount // 2 * 2:2]
    margin = jnp.minimum(sizes[source_of] - 1, most - sizes[receiver]) // 2
    margin = jnp.where((source_of == ranking[0]) | (receiver == ranking[0]) | (sizes[receiver] == 0), 0, jnp.maximum(margin, 0))
    moved = jax.random.randint(jax.random.fold_in(own, 4), (amount // 2,), 0, 1 << 20) % (margin + 1)
    sizes = sizes.at[source_of].add(-moved).at[receiver].add(moved)
    members = jnp.searchsorted(jnp.cumsum(sizes), jnp.arange(rows * top), side="right").astype(jnp.int32)
    grid = members.reshape(top, rows).T
    grid = grid[jax.random.permutation(jax.random.fold_in(own, 1), rows)]
    rotation = jax.random.randint(jax.random.fold_in(own, 2), (rows, 1), 0, top)
    return jnp.take_along_axis(grid, (jnp.arange(top)[None, :] + rotation) % top, axis=1)


def portions_of(number_of, total, most, lean, full):
    loads = [(1 << 20) // math.isqrt(standing ** lean) + 1 for standing in range(1, number_of + 1)]
    largest = most if full else min(most, max(-(-total // number_of), total * loads[0] // sum(loads)))
    least = 1 if total - largest >= number_of - 1 else 0
    holding, spare = [largest] + [least] * (number_of - 1), total - largest - least * (number_of - 1)
    while spare > 0:
        free = [i for i in range(1, number_of) if holding[i] < largest] or [i for i in range(1, number_of) if holding[i] < most]
        whole, left = sum([loads[i] for i in free]), spare
        for i in free:
            more = min(most - holding[i], max(1, left * loads[i] // whole), spare)
            holding[i] = holding[i] + more
            spare = spare - more
    return np.array(holding)


def normal_values(rng, extent, spread, reach, shards=(), kind=jnp.bfloat16):
    values = spread * jax.random.normal(rng, extent, jnp.float32)
    if shards:
        values = values * shard_levels(rng, extent, shards, -0.22, 0.18)
    return jnp.clip(values, -reach, reach).astype(kind)


def setup_inputs(seed: int = 0) -> dict:
    arg_keys = jax.random.split(jax.random.key(seed), 14)
    inputs = normal_values(arg_keys[0], (MICRO, TOKENS, D), 1.0, 6.0, ((1, 16),))
    cotangent = normal_values(arg_keys[1], (MICRO, TOKENS, D), 1.0, 6.0, ((1, 16),))
    seq_lengths = jax.vmap(lambda own: uneven_parts(own, SEQS, PACKED, SEQ_MOST, 2))(jax.random.split(arg_keys[2], MICRO * N_DP)).reshape((MICRO, N_DP, SEQS)).astype(jnp.int32)
    pack_order = jax.vmap(lambda own: jax.random.permutation(own, GROUP_TOK))(jax.random.split(arg_keys[3], MICRO * N_DP)).reshape((MICRO, N_DP, GROUP_TOK)).astype(jnp.int32)
    routes_keys = jax.random.split(jax.random.fold_in(arg_keys[4], 1), MICRO * TOKENS // TOK_DEV)
    routes_turns = jax.random.permutation(jax.random.fold_in(arg_keys[4], 3), MICRO * TOKENS // TOK_DEV)
    routes = jax.vmap(lambda own, number: deal_out(jax.random.fold_in(arg_keys[4], 2), own, number, TOK_DEV, EXPERTS, TOP, CAP, 1))(routes_keys, routes_turns).reshape((MICRO, TOKENS, TOP))
    attn_gain = jnp.clip(1.0 + 0.1 * jax.random.normal(arg_keys[5], (SECTIONS, D), jnp.float32), 0.5, 1.5).astype(jnp.bfloat16)
    w_qkv = normal_values(arg_keys[6], (SECTIONS, D, 3 * D), D ** -0.5, 0.21875, ((0, 2),))
    w_attn_out = normal_values(arg_keys[7], (SECTIONS, D, D), (D // 16) ** -0.5, 0.875, ((0, 2),))
    rel_bias = normal_values(arg_keys[8], (SECTIONS, HEADS, BUCKETS), 1.0, 4.0, ((0, 2),), jnp.float32)
    ffn_gain = jnp.clip(1.0 + 0.1 * jax.random.normal(arg_keys[9], (SECTIONS, D), jnp.float32), 0.5, 1.5).astype(jnp.bfloat16)
    w_router = normal_values(arg_keys[10], (SECTIONS, D, EXPERTS), D ** -0.5, 0.21875, ((0, 2),))
    w_in = normal_values(arg_keys[11], (SECTIONS, EXPERTS, D, FF), D ** -0.5, 0.21875, ((0, 2), (1, 4)))
    w_down = normal_values(arg_keys[12], (SECTIONS, EXPERTS, FF, D), FF ** -0.5, 0.109375, ((0, 2), (1, 4)))
    return {"inputs": inputs, "cotangent": cotangent, "seq_lengths": seq_lengths, "pack_order": pack_order, "routes": routes, "attn_gain": attn_gain, "w_qkv": w_qkv, "w_attn_out": w_attn_out, "rel_bias": rel_bias, "ffn_gain": ffn_gain, "w_router": w_router, "w_in": w_in, "w_down": w_down}


EPSILON = 1e-06
NEGATIVE = -1e+30
PRECISE = lax.Precision.HIGHEST

@jax.custom_vjp
def low(v):
    return lax.optimization_barrier(v.astype(jnp.bfloat16)).astype(jnp.float32)

@jax.custom_vjp
def low_back(v):
    return v

def low_keep(v):
    return (low(v), None)

def low_pass(kept, grad):
    return (grad,)

def back_keep(v):
    return (v, None)

def back_low(kept, grad):
    return (low(grad),)
low.defvjp(low_keep, low_pass)
low_back.defvjp(back_keep, back_low)

def rounded_both(value):
    return low_back(low(value))

def thresholds():
    exact_span = BUCKETS // 2
    values = list(range(1, exact_span))
    for bucket in range(exact_span, BUCKETS):
        values.append(int(math.ceil(exact_span * (MAX_DIST / exact_span) ** ((bucket - exact_span) / exact_span))))
    return values

def bucket_of(distance):
    bucket = jnp.zeros(distance.shape, jnp.int32)
    for limit in thresholds():
        bucket = bucket + (distance >= limit).astype(jnp.int32)
    return bucket

def positions(lengths, pack_pos):
    seq_ends = jnp.cumsum(lengths).astype(jnp.int32)
    passed = pack_pos[:, None] >= seq_ends[None, :]
    segment = lax.optimization_barrier(jnp.sum(passed.astype(jnp.int32), axis=1)).astype(jnp.int32)
    seq_start = lax.optimization_barrier(jnp.sum(jnp.where(passed, lengths[None, :], 0), axis=1)).astype(jnp.int32)
    is_real = segment < lengths.shape[0]
    segment = jnp.where(is_real, segment, lengths.shape[0] + pack_pos).astype(jnp.int32)
    offset = jnp.where(is_real, pack_pos - seq_start, 0).astype(jnp.int32)
    return (segment, offset)

def rms_norm(value, gain):
    return value * lax.rsqrt(lax.optimization_barrier(jnp.mean(value * value, axis=-1, keepdims=True)) + EPSILON) * gain

def gelu_tanh(value):
    return jax.nn.gelu(value, approximate=True)

def attend_group(queries, keys_all, values_all, segment, offset, bias_table):
    slot_count = queries.shape[0]
    block_rows = min(512, slot_count)
    blocks = slot_count // block_rows
    factor = HEAD_DIM ** (-0.5)

    def one_block(block_item):
        block_query, block_segment, block_offset = block_item
        products = jnp.einsum('qhd,khd->hqk', block_query, keys_all, precision=PRECISE) * factor
        distance = block_offset[:, None] - offset[None, :]
        scores = low_back(products + bias_table[:, bucket_of(distance)])
        allowed = (block_segment[:, None] == segment[None, :]) & (distance >= 0)
        masked = jnp.where(allowed[None], scores, NEGATIVE)
        peak = lax.optimization_barrier(jnp.max(masked, axis=2, keepdims=True))
        log_norm = peak + jnp.log(lax.optimization_barrier(jnp.sum(jnp.exp(masked - peak), axis=2, keepdims=True)))
        probs = low(jnp.exp(masked - log_norm))
        return jnp.einsum('hqk,khd->qhd', probs, values_all, precision=PRECISE)
    mixed = lax.map(jax.checkpoint(one_block), (queries.reshape(blocks, block_rows, HEADS, HEAD_DIM), segment.reshape(blocks, block_rows), offset.reshape(blocks, block_rows)))
    return mixed.reshape(slot_count, HEADS * HEAD_DIM)

def layer(stream, weights, lengths, pack_pos, chosen):
    attn_gain, w_qkv, w_attn_out, rel_bias, ffn_gain, w_router, w_in, w_down = weights
    token_count = stream.shape[0]
    normed_low = low(rms_norm(stream, attn_gain))
    projected = rounded_both(jnp.dot(normed_low, w_qkv, precision=PRECISE))
    shaped = projected.reshape(N_DP, GROUP_TOK, 3, HEADS, HEAD_DIM)
    segment, offset = jax.vmap(positions)(lengths, pack_pos)

    def per_group(group_item):
        group_qkv, group_segment, group_offset = group_item
        return attend_group(group_qkv[:, 0], group_qkv[:, 1], group_qkv[:, 2], group_segment, group_offset, rel_bias)
    attended = rounded_both(lax.map(per_group, (shaped, segment, offset)).reshape(token_count, D))
    residual = stream + low_back(jnp.dot(attended, w_attn_out, precision=PRECISE))
    routed_in = low(rms_norm(residual, ffn_gain))
    logits = jnp.dot(routed_in, w_router, precision=PRECISE)
    picked = jnp.take_along_axis(logits, chosen, axis=1)
    gate_peak = lax.optimization_barrier(jnp.max(picked, axis=1, keepdims=True))
    gate_norm = gate_peak + jnp.log(lax.optimization_barrier(jnp.sum(jnp.exp(picked - gate_peak), axis=1, keepdims=True)))
    gates = jnp.exp(picked - gate_norm)
    block_count = token_count // TOK_DEV
    ordered = chosen.reshape(block_count, TOK_DEV, TOP).transpose(0, 2, 1).reshape(block_count, TOP * TOK_DEV)
    onehot = (ordered[:, :, None] == jnp.arange(EXPERTS, dtype=jnp.int32)[None, None, :]).astype(jnp.int32)
    earlier = jnp.cumsum(onehot, axis=1).astype(jnp.int32) - onehot
    place = lax.optimization_barrier(jnp.sum(earlier * onehot, axis=2)).astype(jnp.int32)
    block_ids = jnp.arange(block_count, dtype=jnp.int32)[:, None]
    target = (ordered * block_count + block_ids) * CAP + place
    target = target.reshape(block_count, TOP, TOK_DEV).transpose(0, 2, 1).reshape(token_count * TOP).astype(jnp.int32)
    buffer_rows = jnp.zeros((EXPERTS * block_count * CAP, D), jnp.float32).at[target].set(jnp.repeat(routed_in, TOP, axis=0))
    buffer_rows = low_back(buffer_rows).reshape(EXPERTS, block_count * CAP, D)
    hidden_pre = low_back(jnp.einsum('erd,edf->erf', buffer_rows, w_in, precision=PRECISE))
    activated = low(gelu_tanh(hidden_pre))
    produced = rounded_both(jnp.einsum('erf,efd->erd', activated, w_down, precision=PRECISE)).reshape(EXPERTS * block_count * CAP, D)
    gathered = produced[target].reshape(token_count, TOP, D)
    moe_out = lax.optimization_barrier(jnp.sum(gates[:, :, None] * gathered, axis=1))
    return low(residual + moe_out)

def reference(inputs, cotangent, seq_lengths, pack_order, routes, attn_gain, w_qkv, w_attn_out, rel_bias, ffn_gain, w_router, w_in, w_down):
    params = tuple((member.astype(jnp.float32) for member in (attn_gain, w_qkv, w_attn_out, rel_bias, ffn_gain, w_router, w_in, w_down)))
    stream = inputs.astype(jnp.float32)

    def forward(extra_zero, weights):
        sections = []
        for section_id in range(SECTIONS):
            layer_weights = tuple((member[section_id] for member in weights))
            outputs = []
            for micro_id in range(MICRO):
                if section_id == 0:
                    section_entry = stream[micro_id] + extra_zero[0, micro_id]
                else:
                    section_entry = low_back(sections[section_id - 1][micro_id]) + extra_zero[section_id, micro_id]
                outputs.append(layer(section_entry, layer_weights, seq_lengths[micro_id], pack_order[micro_id], routes[micro_id]))
            sections.append(jnp.stack(outputs))
        return jnp.stack(sections)
    extra_zero = jnp.zeros((SECTIONS,) + stream.shape, jnp.float32)
    result, pullback = jax.vjp(forward, extra_zero, params)
    out_seed = jnp.zeros(result.shape, jnp.float32).at[SECTIONS - 1].set(cotangent.astype(jnp.float32))
    extra_grad, weight_grads = pullback(out_seed)
    return (result.astype(jnp.bfloat16), extra_grad.astype(jnp.bfloat16), weight_grads[0], weight_grads[1], weight_grads[2], weight_grads[3], weight_grads[4], weight_grads[5], weight_grads[6], weight_grads[7])
```

```python
import functools
import math

import jax
import jax.numpy as jnp
import numpy as np
from jax import lax
from jax.experimental import pallas as pl
from jax.experimental.pallas import tpu as pltpu
from jax.sharding import PartitionSpec as P

BUCKETS = 32
MAX_DIST = 128
EPSILON = 1e-06
NEGATIVE = -1e30
PRECISE = lax.Precision.HIGHEST
LANES = 128
F32 = jnp.float32
BF16 = jnp.bfloat16
VM = pl.BlockSpec(memory_space=pltpu.VMEM)
SM = pl.BlockSpec(memory_space=pltpu.SMEM)
ANY = pl.BlockSpec(memory_space=pl.ANY)


def dot(a, b, ca=1, cb=0, precision=None):
    return lax.dot_general(
        a, b, (((ca,), (cb,)), ((), ())), preferred_element_type=F32, precision=precision
    )


def call(kernel, outs, args, specs=None, scratch=(), flops=0, name=None):
    outs = [jax.ShapeDtypeStruct(s, d) for s, d in outs]
    specs = [VM] * len(args) if specs is None else specs
    moved = sum(a.size * a.dtype.itemsize for a in args) + sum(
        math.prod(o.shape) * o.dtype.itemsize for o in outs
    )
    return pl.pallas_call(
        kernel,
        out_shape=outs,
        in_specs=specs,
        out_specs=[VM] * len(outs),
        scratch_shapes=list(scratch),
        cost_estimate=pl.CostEstimate(flops=int(flops), bytes_accessed=int(moved), transcendentals=0),
        compiler_params=pltpu.CompilerParams(vmem_limit_bytes=56 * 1024 * 1024),
        name=name,
    )(*args)


def thresholds():
    exact_span = BUCKETS // 2
    values = list(range(1, exact_span))
    for bucket in range(exact_span, BUCKETS):
        values.append(
            int(
                math.ceil(
                    exact_span * (MAX_DIST / exact_span) ** ((bucket - exact_span) / exact_span)
                )
            )
        )
    return values


def bucket_of(distance):
    bucket = jnp.zeros(distance.shape, jnp.int32)
    for limit in thresholds():
        bucket = bucket + (distance >= limit).astype(jnp.int32)
    return bucket


def diagonal_onehot(tokens):
    distance = (tokens - LANES - np.arange(tokens)) % tokens
    bucket = sum((distance >= limit).astype(np.int64) for limit in thresholds())
    return (np.arange(BUCKETS)[:, None] == bucket[None, :]).astype(np.float32)


def iota(shape, axis):
    return lax.broadcasted_iota(jnp.int32, shape, axis)


def sort_matrix(pack_ref):
    tokens = pack_ref.shape[1]
    return (iota((tokens, tokens), 0) == pack_ref[...]).astype(BF16)


def segment_starts(lengths_ref, tokens):
    place = iota((tokens, 1), 0)
    begin = jnp.zeros((tokens, 1), jnp.int32)
    end = jnp.int32(0)
    for number in range(lengths_ref.shape[0]):
        end = end + lengths_ref[number]
        begin = jnp.where(place >= end, end, begin)
    return jnp.where(place >= end, place, begin)


def diagonals(diag_ref, head, tokens):
    row = jnp.broadcast_to(diag_ref[head : head + 1, :], (LANES, tokens))
    return pltpu.roll(row, 0, 1, stride=1, stride_axis=0)


def attend_forward_kernel(
    heads, size, x_ref, gain_ref, w_ref, diag_ref, lengths_ref, pack_ref,
    normed_ref, qkv_ref, lse_ref, out_ref, sorted_out,
):
    tokens = x_ref.shape[0]
    span = heads * size
    order = sort_matrix(pack_ref)
    x = dot(order, x_ref[...])
    factor = lax.rsqrt(jnp.mean(x * x, axis=1, keepdims=True) + EPSILON)
    normed = (x * factor * gain_ref[...]).astype(BF16)
    normed_ref[...] = normed
    qkv_ref[...] = dot(normed, w_ref[...]).astype(BF16)
    begin = segment_starts(lengths_ref, tokens)
    for head in range(heads):
        bias = diagonals(diag_ref, head, tokens)
        at = head * size
        for block in range(tokens // LANES):
            low, reach = block * LANES, (block + 1) * LANES
            q = qkv_ref[low:reach, at : at + size]
            k = qkv_ref[:reach, span + at : span + at + size]
            v = qkv_ref[:reach, 2 * span + at : 2 * span + at + size]
            column = iota((LANES, reach), 1)
            seen = (column >= begin[low:reach]) & (column <= low + iota((LANES, reach), 0))
            s = dot(q, k, 1, 1) * size ** (-0.5) + bias[:, tokens - reach :]
            s = jnp.where(seen, s, NEGATIVE)
            peak = jnp.max(s, axis=1, keepdims=True)
            e = jnp.exp(s - peak)
            total = jnp.sum(e, axis=1, keepdims=True)
            lse_ref[low:reach, head : head + 1] = peak + jnp.log(total)
            pb = (e * (1.0 / total)).astype(BF16)
            sorted_out[low:reach, at : at + size] = dot(pb, v).astype(BF16)
    out_ref[...] = dot(order, sorted_out[...], 0, 0).astype(BF16)


def attend_backward_kernel(
    heads, size, dproj_ref, wout_ref, att_ref, normed_ref, qkv_ref, lse_ref, w_ref, diag_ref,
    lengths_ref, pack_ref,
    gout_ref, gqkv_ref, dn_ref, gdiag_ref, dkv, dqkv, edge,
):
    tokens, width = dproj_ref.shape
    span = heads * size
    order = sort_matrix(pack_ref)
    dproj = dproj_ref[...]
    do = dot(dproj, wout_ref[...], 1, 1).astype(BF16)
    do = dot(order, do).astype(BF16)
    begin = segment_starts(lengths_ref, tokens)
    gdiag_ref[...] = jnp.zeros(gdiag_ref.shape, F32)
    row_at = iota((LANES, tokens), 0)
    for head in range(heads):
        bias = diagonals(diag_ref, head, tokens)
        at = head * size
        dkv[...] = jnp.zeros(dkv.shape, F32)
        edge[...] = jnp.zeros(edge.shape, F32)
        for block in range(tokens // LANES):
            low, reach = block * LANES, (block + 1) * LANES
            q = qkv_ref[low:reach, at : at + size]
            k = qkv_ref[:reach, span + at : span + at + size]
            v = qkv_ref[:reach, 2 * span + at : 2 * span + at + size]
            dob = do[low:reach, at : at + size]
            column = iota((LANES, reach), 1)
            seen = (column >= begin[low:reach]) & (column <= low + iota((LANES, reach), 0))
            s = dot(q, k, 1, 1) * size ** (-0.5) + bias[:, tokens - reach :]
            s = jnp.where(seen, s, NEGATIVE)
            p = jnp.exp(s - lse_ref[low:reach, head : head + 1])
            dp = dot(dob, v, 1, 1)
            delta = jnp.sum(p * dp, axis=1, keepdims=True)
            ds = (p * (dp - delta)).astype(BF16)
            dqkv[low:reach, at : at + size] = (dot(ds, k) * size ** (-0.5)).astype(BF16)
            dkv[0, :reach, :] += dot(ds, q, 0, 0)
            dkv[1, :reach, :] += dot(p.astype(BF16), dob, 0, 0)
            edge[:, tokens - reach :] += ds.astype(F32)
        dqkv[:, span + at : span + at + size] = (dkv[0] * size ** (-0.5)).astype(BF16)
        dqkv[:, 2 * span + at : 2 * span + at + size] = dkv[1].astype(BF16)
        skew = edge[...]
        step = 1
        while step < LANES:
            moved = pltpu.roll(skew, tokens - step, 1)
            skew = jnp.where((row_at & step) != 0, moved, skew)
            step *= 2
        gdiag_ref[head : head + 1, :] = jnp.sum(skew, axis=0, keepdims=True)
    d = dqkv[...]
    gqkv_ref[...] = dot(normed_ref[...], d, 0, 0).astype(BF16)
    gout_ref[...] = dot(att_ref[...], dproj, 0, 0).astype(BF16)
    dn = dot(d, w_ref[...], 1, 1).astype(BF16)
    dn_ref[...] = dot(order, dn, 0, 0).astype(BF16)


def routing(chosen, expert_total, capacity):
    top_count = chosen.shape[1]
    flat = jnp.concatenate([chosen[:, k] for k in range(top_count)])[None, :]
    onehot = jnp.arange(expert_total, dtype=jnp.int32)[:, None] == flat
    count = flat.shape[1]
    before = jnp.asarray(np.triu(np.ones((count, count), np.float32), 1), BF16)
    earlier = jnp.dot(onehot.astype(BF16), before, preferred_element_type=F32)
    place = jnp.sum(jnp.where(onehot, earlier, 0.0), axis=0, keepdims=True).astype(jnp.int32)
    return flat * capacity + place


def selects(target_ref, slots):
    rows = target_ref.shape[1] // 2
    at = iota((slots, rows), 0)
    return [(at == target_ref[:, k * rows : (k + 1) * rows]).astype(BF16) for k in range(2)]


def both(pair):
    return (pair[0].astype(F32) + pair[1].astype(F32)).astype(BF16)


def after_attention_kernel(
    part_ref, x_ref, wout_ref, gain_ref, router_ref, chosen_ref, target_ref,
    residual_ref, normed_ref, gates_ref, sent_ref,
):
    parts, rows, span = part_ref.shape
    mixed = dot(part_ref[0], wout_ref[:span, :])
    for number in range(1, parts):
        mixed += dot(part_ref[number], wout_ref[number * span : (number + 1) * span, :])
    residual = x_ref[...].astype(F32) + mixed
    residual_ref[...] = residual
    factor = lax.rsqrt(jnp.mean(residual * residual, axis=1, keepdims=True) + EPSILON)
    normed = (residual * factor * gain_ref[...]).astype(BF16)
    normed_ref[...] = normed
    logits = dot(normed, router_ref[...])
    lane = iota(logits.shape, 1)
    z = [
        jnp.sum(jnp.where(lane == chosen_ref[:, k : k + 1], logits, 0.0), axis=1, keepdims=True)
        for k in range(2)
    ]
    peak = jnp.maximum(z[0], z[1])
    norm = peak + jnp.log(jnp.exp(z[0] - peak) + jnp.exp(z[1] - peak))
    gates_ref[...] = jnp.where(
        lane == 0, jnp.exp(z[0] - norm), jnp.where(lane == 1, jnp.exp(z[1] - norm), 0.0)
    )
    sent_ref[...] = dot(both(selects(target_ref, sent_ref.shape[0])), normed).astype(BF16)


def combine_kernel(residual_ref, gates_ref, returned_ref, target_ref, out_ref):
    total = residual_ref[...]
    returned = returned_ref[...]
    for k, select in enumerate(selects(target_ref, returned.shape[0])):
        total += gates_ref[:, k : k + 1] * dot(select, returned, 0, 0)
    out_ref[...] = total.astype(BF16)


def rows_backward_kernel(
    grad_ref, gates_ref, returned_ref, target_ref, chosen_ref, normed_ref,
    scattered_ref, dlogits_ref, grouter_ref,
):
    grad = grad_ref[...].astype(F32)
    returned = returned_ref[...]
    pair = selects(target_ref, returned.shape[0])
    gates = [gates_ref[:, k : k + 1] for k in range(2)]
    dg = [jnp.sum(grad * dot(pair[k], returned, 0, 0), axis=1, keepdims=True) for k in range(2)]
    mean = gates[0] * dg[0] + gates[1] * dg[1]
    lane = iota(dlogits_ref.shape, 1)
    dlogits = jnp.zeros(dlogits_ref.shape, F32)
    for k in range(2):
        dlogits += jnp.where(lane == chosen_ref[:, k : k + 1], gates[k] * (dg[k] - mean), 0.0)
    dlogits_ref[...] = dlogits
    grouter_ref[...] = dot(normed_ref[...].astype(F32), dlogits, 0, 0, PRECISE)
    scattered_ref[...] = (
        dot(pair[0], (gates[0] * grad).astype(BF16)) + dot(pair[1], (gates[1] * grad).astype(BF16))
    ).astype(BF16)


def norm_backward(value, gain, grad):
    factor = lax.rsqrt(jnp.mean(value * value, axis=1, keepdims=True) + EPSILON)
    scaled = grad * gain
    value_grad = factor * scaled - value * (factor * factor * factor) * jnp.mean(
        scaled * value, axis=1, keepdims=True
    )
    return value_grad, jnp.sum(grad * value * factor, axis=0, keepdims=True)


def residual_backward_kernel(
    returned_ref, target_ref, dlogits_ref, router_ref, residual_ref, gain_ref, grad_ref,
    dres_ref, dproj_ref, ggain_ref,
):
    select = both(selects(target_ref, returned_ref.shape[0]))
    dnormed = dot(select, returned_ref[...], 0, 0) + dot(
        dlogits_ref[...], router_ref[...].astype(F32), 1, 1, PRECISE
    )
    value_grad, ggain_ref[...] = norm_backward(residual_ref[...], gain_ref[...], dnormed)
    dres = grad_ref[...].astype(F32) + value_grad
    dres_ref[...] = dres
    dproj_ref[...] = dres.astype(BF16)


def input_backward_kernel(part_ref, x_ref, gain_ref, dres_ref, out_ref, ggain_ref):
    dnormed = part_ref[0].astype(F32)
    for number in range(1, part_ref.shape[0]):
        dnormed += part_ref[number].astype(F32)
    value_grad, ggain_ref[...] = norm_backward(x_ref[...].astype(F32), gain_ref[...], dnormed)
    out_ref[...] = (dres_ref[...] + value_grad).astype(BF16)


GELU_C = math.sqrt(2.0 / math.pi)
GELU_A = 0.044715


def gelu_parts(x):
    square = x * x
    half = 0.5 + 0.5 * jnp.tanh(x * (GELU_C + (GELU_C * GELU_A) * square))
    act = x * half
    slope = half + act * (1.0 - half) * (2 * GELU_C + (6 * GELU_C * GELU_A) * square)
    return act, slope


def fetch(pick_ref, choices, buffer, sem):
    for number, source in enumerate(choices):

        @pl.when(pick_ref[0] == number)
        def _():
            pltpu.make_async_copy(source, buffer, sem).start()


def arrive(source, buffer, sem):
    pltpu.make_async_copy(source, buffer, sem).wait()


def tile_of(hidden):
    return 512 if hidden % 512 == 0 else hidden


def experts_forward_kernel(
    pick_ref, rows_ref, in_a, in_b, down_a, down_b, out_ref, slope_ref, in_buf, down_buf, acc, sem
):
    tiles, _, tile = in_buf.shape
    for number in range(tiles):
        cut = pl.ds(number * tile, tile)
        fetch(pick_ref, (in_a.at[:, cut], in_b.at[:, cut]), in_buf.at[number], sem.at[0, number])
        fetch(pick_ref, (down_a.at[cut], down_b.at[cut]), down_buf.at[number], sem.at[1, number])
    rows = rows_ref[...]
    for number in range(tiles):
        cut = pl.ds(number * tile, tile)
        arrive(in_a.at[:, cut], in_buf.at[number], sem.at[0, number])
        act, slope = gelu_parts(dot(rows, in_buf[number]))
        slope_ref[:, number * tile : (number + 1) * tile] = slope.astype(BF16)
        arrive(down_a.at[cut], down_buf.at[number], sem.at[1, number])
        part = dot(act.astype(BF16), down_buf[number])
        if number == 0:
            acc[...] = part
        else:
            acc[...] += part
    out_ref[...] = acc[...].astype(BF16)


def experts_backward_kernel(
    pick_ref, rows_ref, slope_ref, in_a, in_b, down_a, down_b, out_ref, in_buf, down_buf, acc, sem
):
    tiles, _, tile = in_buf.shape
    for number in range(tiles):
        cut = pl.ds(number * tile, tile)
        fetch(pick_ref, (down_a.at[cut], down_b.at[cut]), down_buf.at[number], sem.at[1, number])
        fetch(pick_ref, (in_a.at[:, cut], in_b.at[:, cut]), in_buf.at[number], sem.at[0, number])
    rows = rows_ref[...]
    for number in range(tiles):
        cut = pl.ds(number * tile, tile)
        arrive(down_a.at[cut], down_buf.at[number], sem.at[1, number])
        slope = slope_ref[:, number * tile : (number + 1) * tile].astype(F32)
        dpre = (slope * dot(rows, down_buf[number], 1, 1)).astype(BF16)
        arrive(in_a.at[:, cut], in_buf.at[number], sem.at[0, number])
        part = dot(dpre, in_buf[number], 1, 1)
        if number == 0:
            acc[...] = part
        else:
            acc[...] += part
    out_ref[...] = acc[...].astype(BF16)


def experts_weights_kernel(
    pick_ref, place_ref, rows_ref, grads_ref, in_a, in_b, down_a, down_b, gin_ref, gdown_ref,
    in_buf, down_buf, gin, gdown, sem,
):
    part = in_buf.shape[1]
    cut = pl.ds(pl.multiple_of(place_ref[0] * part, LANES), part)
    fetch(pick_ref, (in_a.at[:, cut], in_b.at[:, cut]), in_buf, sem.at[0])
    fetch(pick_ref, (down_a.at[cut], down_b.at[cut]), down_buf, sem.at[1])
    gin[...] = jnp.zeros(gin.shape, F32)
    gdown[...] = jnp.zeros(gdown.shape, F32)
    arrive(in_a.at[:, cut], in_buf, sem.at[0])
    arrive(down_a.at[cut], down_buf, sem.at[1])

    def chunk(number, carry):
        rows = rows_ref[number]
        grads = grads_ref[number]
        act, slope = gelu_parts(dot(rows, in_buf[...]))
        dpre = (slope * dot(grads, down_buf[...], 1, 1)).astype(BF16)
        gdown[...] += dot(act.astype(BF16), grads, 0, 0)
        gin[...] += dot(rows, dpre, 0, 0)
        return carry

    lax.fori_loop(0, rows_ref.shape[0], chunk, 0)
    gin_ref[...] = gin[...].astype(BF16)
    gdown_ref[...] = gdown[...].astype(BF16)


def positions(lengths, pack_pos):
    seq_ends = jnp.cumsum(lengths)
    passed = pack_pos[:, None] >= seq_ends[None, :]
    segment = jnp.sum(passed.astype(jnp.int32), axis=1)
    seq_start = jnp.sum(jnp.where(passed, lengths[None, :], 0), axis=1)
    is_real = segment < lengths.shape[0]
    segment = jnp.where(is_real, segment, lengths.shape[0] + pack_pos)
    offset = jnp.where(is_real, pack_pos - seq_start, 0)
    return (segment, offset)


def plain_context(lengths, pack_pos, expert_index, row_count):
    segment, offset = positions(lengths, pack_pos)
    q_segment = lax.dynamic_slice_in_dim(segment, expert_index * row_count, row_count)
    q_offset = lax.dynamic_slice_in_dim(offset, expert_index * row_count, row_count)
    distance = q_offset[:, None] - offset[None, :]
    allowed = (q_segment[:, None] == segment[None, :]) & (distance >= 0)
    return bucket_of(distance), allowed


def plain_scores(queries, gathered, context, rel_bias):
    bucket, allowed = context
    rows, width = queries.shape
    heads = rel_bias.shape[0]
    size = width // heads
    q = queries.reshape(rows, heads, size)
    k = gathered[:, :width].reshape(-1, heads, size)
    s = jnp.einsum("qhd,khd->hqk", q, k, preferred_element_type=F32) * size ** (-0.5)
    return jnp.where(allowed[None], s + rel_bias[:, bucket], NEGATIVE)


def plain_forward(x, gain, w_qkv, rel_bias, context):
    rows, width = x.shape
    heads = rel_bias.shape[0]
    value = x.astype(F32)
    factor = lax.rsqrt(jnp.mean(value * value, axis=-1, keepdims=True) + EPSILON)
    normed = (value * factor * gain).astype(BF16)
    projected = jnp.dot(normed, w_qkv, preferred_element_type=F32).astype(BF16)
    queries, keyval = projected[:, :width], projected[:, width:]
    gathered = lax.all_gather(keyval, "expert", axis=0, tiled=True)
    s = plain_scores(queries, gathered, context, rel_bias)
    lse = jax.nn.logsumexp(s, axis=2)
    probs = jnp.exp(s - lse[:, :, None]).astype(BF16)
    v = gathered[:, width:].reshape(-1, heads, width // heads)
    mixed = jnp.einsum("hqk,khd->qhd", probs, v, preferred_element_type=F32)
    return mixed.reshape(rows, width).astype(BF16), (normed, queries, gathered, lse)


def plain_backward(dproj, attended, saved, w_qkv, w_out, rel_bias, context):
    normed, queries, gathered, lse = saved
    rows, width = dproj.shape
    heads = rel_bias.shape[0]
    size = width // heads
    factor = size ** (-0.5)
    gout = jnp.einsum("td,te->de", attended, dproj, preferred_element_type=F32)
    do = jnp.einsum("te,de->td", dproj, w_out, preferred_element_type=F32).astype(BF16)
    do = do.reshape(rows, heads, size)
    q = queries.reshape(rows, heads, size)
    k = gathered[:, :width].reshape(-1, heads, size)
    v = gathered[:, width:].reshape(-1, heads, size)
    s = plain_scores(queries, gathered, context, rel_bias)
    probs = jnp.exp(s - lse[:, :, None])
    dp = jnp.einsum("qhd,khd->hqk", do, v, preferred_element_type=F32)
    delta = jnp.sum(probs * dp, axis=2)
    ds = (probs * (dp - delta[:, :, None])).astype(BF16)
    dq = jnp.einsum("hqk,khd->qhd", ds, k, preferred_element_type=F32) * factor
    dk = jnp.einsum("hqk,qhd->khd", ds, q, preferred_element_type=F32) * factor
    dv = jnp.einsum("hqk,qhd->khd", probs.astype(BF16), do, preferred_element_type=F32)
    hot = (context[0][:, :, None] == jnp.arange(BUCKETS, dtype=jnp.int32)).astype(BF16)
    gtable = jnp.einsum("hqk,qkb->hb", ds, hot, preferred_element_type=F32)
    update = jnp.concatenate([dk.reshape(-1, width), dv.reshape(-1, width)], axis=1)
    own = lax.psum_scatter(update.astype(BF16), "expert", scatter_dimension=0, tiled=True)
    grads = jnp.concatenate([dq.reshape(rows, width).astype(BF16), own], axis=1)
    gqkv = jnp.einsum("td,te->de", normed, grads, preferred_element_type=F32)
    dn = jnp.einsum("te,de->td", grads, w_qkv, preferred_element_type=F32).astype(BF16)
    return dn, gout, gqkv, gtable


def exchange(value, axis="section"):
    return lax.ppermute(value, axis, [(0, 1), (1, 0)])


def handed(value, source):
    return lax.ppermute(value, "section", [(source, 1 - source)])


def within(value, layer, axis, pairs):
    count = lax.axis_size(axis)
    base = layer * count
    return lax.ppermute(value, ("section", axis), [(base + a, base + b) for a, b in pairs])


def spread(piece, layer, axis):
    count = lax.axis_size(axis)
    me = lax.axis_index(axis)
    out = jnp.zeros((count,) + piece.shape, piece.dtype)
    out = lax.dynamic_update_index_in_dim(out, piece, me, 0)
    for step in range(1, count):
        got = within(piece, layer, axis, [(a, (a + step) % count) for a in range(count)])
        out = lax.dynamic_update_index_in_dim(out, got, lax.rem(me - step + count, count), 0)
    return out


def gather_sum(total, layer):
    count = lax.axis_size("dp")
    me = lax.axis_index("dp")
    cuts = total.reshape(count, total.shape[0] // count, total.shape[1])
    mine = lax.dynamic_index_in_dim(cuts, me, 0, keepdims=False).astype(F32)
    for step in range(1, count):
        out = lax.dynamic_index_in_dim(cuts, lax.rem(me + step, count), 0, keepdims=False)
        got = within(out.astype(BF16), layer, "dp", [(a, (a + step) % count) for a in range(count)])
        mine = mine + got.astype(F32)
    column = spread(mine.astype(BF16), layer, "dp").reshape(total.shape)
    return spread(column, layer, "expert")


def body(
    inputs, cotangent, seq_lengths, pack_order, routes, attn_gain, w_qkv, w_attn_out, rel_bias,
    ffn_gain, w_router, w_in, w_down,
):
    section = lax.axis_index("section")
    expert = lax.axis_index("expert")
    dp = lax.axis_index("dp")
    n_expert = lax.axis_size("expert")
    n_dp = lax.axis_size("dp")
    layers = 2
    first = section == 0
    rows, width = inputs.shape[1:]
    heads = rel_bias.shape[1]
    size = width // heads
    expert_total = w_router.shape[2]
    hidden = w_in.shape[3]
    tokens = rows * n_expert
    capacity = 5 * rows // (2 * expert_total)
    slots = expert_total * capacity
    headed = heads % n_expert == 0 and tokens % LANES == 0 and tokens <= 1024
    local = heads // n_expert if headed else heads
    span = local * size

    def mine(array):
        return lax.dynamic_index_in_dim(array, section, 0, keepdims=False)

    x_own = mine(inputs)
    cot = mine(cotangent)
    lengths = mine(seq_lengths)[0]
    pack = mine(pack_order)[0]
    chosen = mine(routes)

    x_all = lax.all_gather(x_own, "expert", axis=0, tiled=True) if headed else None
    if headed:
        cut = w_qkv[0].reshape(width, 3, n_expert, span)
        qkv_own = lax.dynamic_index_in_dim(cut, expert, 2, keepdims=False).reshape(width, 3 * span)
    else:
        qkv_own = w_qkv[0]
    small_own = jnp.concatenate(
        [
            attn_gain[0].astype(F32),
            ffn_gain[0].astype(F32),
            w_router[0].astype(F32).reshape(-1),
            rel_bias[0].reshape(-1),
        ]
    )
    small_other = exchange(small_own)
    qkv_other = exchange(qkv_own)
    out_own = w_attn_out[0]
    out_other = exchange(out_own)
    in_own, down_own = w_in[0, 0], w_down[0, 0]
    in_other = exchange(in_own)
    down_other = exchange(down_own)

    def of_layer(layer, own, other):
        return jnp.where(section == layer, own, other)

    weights = []
    for layer in range(layers):
        small = of_layer(layer, small_own, small_other)
        at = 2 * width
        router = small[at : at + width * expert_total].reshape(width, expert_total).astype(BF16)
        table = small[at + width * expert_total :].reshape(heads, BUCKETS)
        weights.append(
            {
                "attn_gain": small[None, :width],
                "ffn_gain": small[None, width : 2 * width],
                "router": jnp.pad(router, ((0, 0), (0, LANES - expert_total))),
                "table": table,
                "qkv": of_layer(layer, qkv_own, qkv_other),
                "out": of_layer(layer, out_own, out_other),
                "pick": jnp.where(section == layer, 0, 1).astype(jnp.int32).reshape(1),
                "experts": (in_own, in_other, down_own, down_other),
            }
        )

    target = routing(chosen, expert_total, capacity)
    if headed:
        onehot = jnp.asarray(diagonal_onehot(tokens))
        pack_row = pack[None, :]
    else:
        context = plain_context(lengths, pack, expert, rows)

    def to_experts(value):
        return lax.all_to_all(
            value.reshape(n_expert, -1, width), "expert", split_axis=0, concat_axis=0, tiled=True
        ).reshape(slots, width)

    tile = tile_of(hidden)
    tiles = hidden // tile
    expert_specs = [SM, VM, ANY, ANY, ANY, ANY]
    expert_scratch = [
        pltpu.VMEM((tiles, width, tile), BF16),
        pltpu.VMEM((tiles, tile, width), BF16),
        pltpu.VMEM((slots, width), F32),
        pltpu.SemaphoreType.DMA((2, tiles)),
    ]
    expert_flops = 4 * slots * width * hidden

    def forward(layer, x, x_all):
        w = weights[layer]
        kept = {"x": x}
        if headed:
            table = lax.dynamic_slice_in_dim(w["table"], expert * local, local, 0)
            diag = jnp.dot(table, onehot, precision=PRECISE)
            kept["diag"] = jnp.pad(diag, ((0, -local % 8), (0, 0)))
            kept["normed"], kept["qkv"], kept["lse"], att = call(
                functools.partial(attend_forward_kernel, local, size),
                [
                    ((tokens, width), BF16),
                    ((tokens, 3 * span), BF16),
                    ((tokens, LANES), F32),
                    ((tokens, span), BF16),
                ],
                [x_all, w["attn_gain"], w["qkv"], kept["diag"], lengths, pack_row],
                [VM, VM, VM, VM, SM, VM],
                [pltpu.VMEM((tokens, span), BF16)],
                flops=2 * tokens * width * (3 * span + tokens),
                name="attend_forward",
            )
            kept["att"] = att
            parts = lax.all_to_all(
                att.reshape(n_expert, rows, span), "expert", split_axis=0, concat_axis=0, tiled=True
            )
        else:
            att, kept["plain"] = plain_forward(x, w["attn_gain"], w["qkv"], w["table"], context)
            kept["att"] = att
            parts = att[None]
        kept["residual"], kept["normed_two"], kept["gates"], sent = call(
            after_attention_kernel,
            [((rows, width), F32), ((rows, width), BF16), ((rows, LANES), F32), ((slots, width), BF16)],
            [parts, x, w["out"], w["ffn_gain"], w["router"], chosen, target],
            flops=2 * rows * width * (width + slots),
            name="after_attention",
        )
        received = to_experts(sent)
        kept["received"] = lax.all_gather(received, "dp", axis=0, tiled=False)
        produced, kept["slope"] = call(
            experts_forward_kernel,
            [((slots, width), BF16), ((slots, hidden), BF16)],
            [w["pick"], received, *w["experts"]],
            expert_specs,
            expert_scratch,
            flops=expert_flops,
            name="experts_forward",
        )
        kept["returned"] = to_experts(produced)
        out = call(
            combine_kernel,
            [((rows, width), BF16)],
            [kept["residual"], kept["gates"], kept["returned"], target],
            flops=4 * rows * width * slots,
            name="combine",
        )[0]
        return out, kept

    def backward(layer, grad, kept):
        w = weights[layer]
        scattered, dlogits, grouter = call(
            rows_backward_kernel,
            [((slots, width), BF16), ((rows, LANES), F32), ((width, LANES), F32)],
            [grad, kept["gates"], kept["returned"], target, chosen, kept["normed_two"]],
            flops=8 * rows * width * slots,
            name="rows_backward",
        )
        arrived = to_experts(scattered)
        all_arrived = lax.all_gather(arrived, "dp", axis=0, tiled=False)
        back = call(
            experts_backward_kernel,
            [((slots, width), BF16)],
            [w["pick"], arrived, kept["slope"], *w["experts"]],
            [SM, VM, VM, ANY, ANY, ANY, ANY],
            expert_scratch,
            flops=expert_flops,
            name="experts_backward",
        )[0]
        returned = to_experts(back)
        dres, dproj, gffn = call(
            residual_backward_kernel,
            [((rows, width), F32), ((rows, width), BF16), ((1, width), F32)],
            [returned, target, dlogits, w["router"], kept["residual"], w["ffn_gain"], grad],
            flops=2 * rows * width * slots,
            name="residual_backward",
        )
        part = hidden // n_dp
        gin, gdown = call(
            experts_weights_kernel,
            [((width, part), BF16), ((part, width), BF16)],
            [w["pick"], dp.astype(jnp.int32).reshape(1), kept["received"], all_arrived, *w["experts"]],
            [SM, SM, VM, VM, ANY, ANY, ANY, ANY],
            [
                pltpu.VMEM((width, part), BF16),
                pltpu.VMEM((part, width), BF16),
                pltpu.VMEM((width, part), F32),
                pltpu.VMEM((part, width), F32),
                pltpu.SemaphoreType.DMA((2,)),
            ],
            flops=2 * expert_flops,
            name="experts_weights",
        )
        if headed:
            dproj_all = lax.all_gather(dproj, "expert", axis=0, tiled=True)
            out_rows = lax.dynamic_slice_in_dim(w["out"], expert * span, span, 0)
            gout, gqkv, dn, gdiag = call(
                functools.partial(attend_backward_kernel, local, size),
                [
                    ((span, width), BF16),
                    ((width, 3 * span), BF16),
                    ((tokens, width), BF16),
                    ((kept["diag"].shape[0], tokens), F32),
                ],
                [
                    dproj_all, out_rows, kept["att"], kept["normed"], kept["qkv"], kept["lse"],
                    w["qkv"], kept["diag"], lengths, pack_row,
                ],
                [VM] * 8 + [SM, VM],
                [
                    pltpu.VMEM((2, tokens, size), F32),
                    pltpu.VMEM((tokens, 3 * span), BF16),
                    pltpu.VMEM((LANES, tokens), F32),
                ],
                flops=2 * tokens * width * (7 * span + tokens),
                name="attend_backward",
            )
            parts = lax.all_to_all(
                dn.reshape(n_expert, rows, width), "expert", split_axis=0, concat_axis=0, tiled=True
            )
            gtable = jnp.dot(gdiag[:local], onehot.T, precision=PRECISE)
            gtable = lax.dynamic_update_slice_in_dim(
                jnp.zeros((heads, BUCKETS), F32), gtable, expert * local, 0
            )
            dense = jnp.concatenate([gout, gqkv.T], axis=0)
            dense = dense.astype(F32) + handed(dense, 1 - layer).astype(F32)
            dense = gather_sum(dense, layer)
        else:
            dn, gout, gqkv, gtable = plain_backward(
                dproj, kept["att"], kept["plain"], w["qkv"], w["out"], w["table"], context
            )
            parts = dn[None]
            dense = lax.psum(jnp.concatenate([gout, gqkv], axis=1), ("section", "dp", "expert"))
        in_grad, gattn = call(
            input_backward_kernel,
            [((rows, width), BF16), ((1, width), F32)],
            [parts, kept["x"], w["attn_gain"], dres],
            name="input_backward",
        )
        little = jnp.concatenate(
            [gattn[0], gffn[0], grouter[:, :expert_total].reshape(-1), gtable.reshape(-1)]
        )
        return in_grad, (gin, gdown, dense, little)

    acts0, kept0 = forward(0, x_own, x_all)
    acts0_all = lax.all_gather(acts0, "expert", axis=0, tiled=True) if headed else None
    acts1, kept1 = forward(1, acts0, acts0_all)
    grad1, grads1 = backward(1, cot, kept1)
    grad0, grads0 = backward(0, grad1, kept0)

    def placed(value0, value1):
        own = jnp.where(first, value0, value1)
        got = exchange(jnp.where(first, value1, value0))
        return jnp.where(
            first, jnp.stack([own, got]), jnp.stack([got, own])
        )

    def summed(index):
        own = jnp.where(first, grads0[index], grads1[index])
        got = exchange(jnp.where(first, grads1[index], grads0[index]))
        return own.astype(F32) + got.astype(F32)

    gin = summed(0).astype(BF16)
    gin = lax.all_to_all(
        gin.reshape(n_dp, width // n_dp, hidden // n_dp), "dp", split_axis=0, concat_axis=0, tiled=True
    )
    gin = jnp.transpose(gin.astype(F32), (1, 0, 2)).reshape(width // n_dp, hidden)
    gdown = summed(1)

    dense = jnp.where(first, grads0[2], grads1[2])
    if headed:
        gout = dense[:, :span].reshape(width, width).astype(F32)
        gqkv = dense[:, span:].reshape(n_expert, 3, span, width)
        gqkv = jnp.transpose(gqkv, (3, 1, 0, 2)).reshape(width, 3 * width).astype(F32)
    else:
        gout, gqkv = dense[:, :width], dense[:, width:]

    little = lax.psum(jnp.stack([grads0[3], grads1[3]]), ("section", "dp", "expert"))
    little = jnp.where(first, little[0], little[1])
    at = 2 * width
    grouter = little[at : at + width * expert_total].reshape(width, expert_total)
    gtable = little[at + width * expert_total :].reshape(heads, BUCKETS)

    return (
        placed(acts0, acts1)[None],
        placed(grad0, grad1)[None],
        little[None, :width],
        gqkv[None],
        gout[None],
        gtable[None],
        little[None, width : 2 * width],
        grouter[None],
        gin[None, None],
        gdown[None, None],
    )


def solution(mesh):
    return jax.shard_map(
        body,
        mesh=mesh,
        in_specs=(
            P(None, ("dp", "expert"), None),
            P(None, ("dp", "expert"), None),
            P(None, "dp", None),
            P(None, "dp", None),
            P(None, ("dp", "expert"), None),
            P("section", None),
            P("section", None, None),
            P("section", None, None),
            P("section", None, None),
            P("section", None),
            P("section", None, None),
            P("section", "expert", None, None),
            P("section", "expert", None, None),
        ),
        out_specs=(
            P("section", None, ("dp", "expert"), None),
            P("section", None, ("dp", "expert"), None),
            P("section", None),
            P("section", None, None),
            P("section", None, None),
            P("section", None, None),
            P("section", None),
            P("section", None, None),
            P("section", "expert", "dp", None),
            P("section", "expert", "dp", None),
        ),
        check_vma=False,
    )
```
